32 devices in a mesh: grp: 4 (over y, x), ext: 8 (over z, core).
Axes of the slice: x: 2, y: 2, z: 4, core: 2. Of those that a mesh axis runs over, the one named last changes fastest.
Arguments:
- tiles: bfloat16 [576, 49, 2048], P(('grp', 'ext')), may hold values from -6 to 6
- tissue_index: int32 [32, 18], P(('grp', 'ext')), may hold values from 0 to 17, each once within a row
- tissue_count: int32 [32], P(('grp', 'ext')), may hold values from 0 to 16, as said below
- w_reduce: bfloat16 [2048, 512], replicated, may hold values from -0.125 to 0.125
- scale_reduce: float32 [512], replicated, may hold values from 0.5 to 2
- bias_reduce: float32 [512], replicated, may hold values from -3 to 3
- w_spatial: bfloat16 [3, 3, 512, 512], replicated, may hold values from -0.09375 to 0.09375
- scale_spatial: float32 [512], replicated, may hold values from 0.5 to 2
- bias_spatial: float32 [512], replicated, may hold values from -3 to 3
- w_expand: bfloat16 [512, 2048], replicated, may hold values from -0.25 to 0.25
- scale_expand: float32 [2048], replicated, may hold values from 0.5 to 2
- bias_expand: float32 [2048], replicated, may hold values from -3 to 3
Outputs:
- embeddings: bfloat16 [256, 2048], P(('grp', 'ext'))
The draws below stay inside these ranges and needn't reach their ends.
Inputs may be any that keep to these rules, and one draw needn't show every extreme that they name: Let S(d) be the sum of tissue_count over owners before owner d; then 8 * d <= S(d) <= 8 * (d + 1) for every d, and all counts sum to 256.
All inputs are finite; a program needn't handle non-finite values.
Results may differ from the reference program's by a relative error of at most 0.0021.
Values may be sent and summed in bfloat16 or wider, within the bound.
No kernel may reach another device: no remote copies, remote signals or barrier semaphores. Data moves between devices by JAX's collectives and lax.ppermute only.
A program may use at most 128 MiB of HBM per device.

```python
import math
import jax
import jax.numpy as jnp
from jax import lax

C = 2048
MID = 512
SIDE = 7
SEQ_DEV = 8
CAND = 18
OWNERS = 32
TOTAL = 256


def draw_tissue_count(key, part):
    drift_key = jax.random.fold_in(key, 11)
    drift_vals = jax.random.randint(drift_key, (OWNERS + 1,), 1, SEQ_DEV + 1, dtype=jnp.int32)
    drift_vals = drift_vals.at[1].set(SEQ_DEV).at[OWNERS - 1].set(SEQ_DEV)
    drift_vals = drift_vals.at[0].set(0).at[OWNERS].set(0)
    return (SEQ_DEV + drift_vals[1:] - drift_vals[:-1]).astype(jnp.int32)


def block_levels(own_key, extent, shards, least, largest):
    def one(dim, parts):
        draws = jax.random.uniform(jax.random.fold_in(jax.random.fold_in(own_key, 6), dim), (parts,), jnp.float32, least / len(shards), largest / len(shards))
        return jnp.repeat(jnp.exp(draws), extent[dim] // parts).reshape((-1,) + (1,) * (len(extent) - dim - 1))

    gain = one(*shards[0])
    for cut in shards[1:]:
        gain = gain * one(*cut)
    return gain


def gaussian(own_key, extent, spread, reach, shards=(), kind=jnp.bfloat16):
    array = jax.random.normal(own_key, extent, jnp.float32) * spread
    if len(shards) > 0:
        array = block_levels(own_key, extent, shards, -0.22, 0.18) * array
    return jnp.clip(array, min=-reach, max=reach).astype(kind)


def setup_inputs(seed: int = 0) -> dict:
    seeds = jax.random.split(jax.random.key(seed), 13)
    tiles = gaussian(seeds[0], (OWNERS * CAND, SIDE * SIDE, C), 1.0, 6.0, ((0, 32),))
    tissue_index = jax.vmap(lambda own: jax.random.permutation(own, CAND))(jax.random.split(seeds[1], OWNERS)).reshape((OWNERS, CAND)).astype(jnp.int32)
    tissue_count = draw_tissue_count(jax.random.fold_in(seeds[12], 71), 0)
    w_reduce = gaussian(seeds[3], (C, MID), C ** -0.5, 0.125)
    scale_reduce = jnp.clip(jnp.exp(jax.random.uniform(seeds[4], (MID,), jnp.float32, math.log(0.5), math.log(2.0))), 0.5, 2.0)
    bias_reduce = gaussian(seeds[5], (MID,), 0.5, 3.0, (), jnp.float32)
    w_spatial = gaussian(seeds[6], (3, 3, MID, MID), (9 * MID) ** -0.5, 0.09375)
    scale_spatial = jnp.clip(jnp.exp(jax.random.uniform(seeds[7], (MID,), jnp.float32, math.log(0.5), math.log(2.0))), 0.5, 2.0)
    bias_spatial = gaussian(seeds[8], (MID,), 0.5, 3.0, (), jnp.float32)
    w_expand = gaussian(seeds[9], (MID, C), MID ** -0.5, 0.25)
    scale_expand = jnp.clip(jnp.exp(jax.random.uniform(seeds[10], (C,), jnp.float32, math.log(0.5), math.log(2.0))), 0.5, 2.0)
    bias_expand = gaussian(seeds[11], (C,), 0.5, 3.0, (), jnp.float32)
    return dict(tiles=tiles, tissue_index=tissue_index, tissue_count=tissue_count, w_reduce=w_reduce, scale_reduce=scale_reduce, bias_reduce=bias_reduce, w_spatial=w_spatial, scale_spatial=scale_spatial, bias_spatial=bias_spatial, w_expand=w_expand, scale_expand=scale_expand, bias_expand=bias_expand)


def bottleneck(tile_maps, w_reduce, scale_reduce, bias_reduce, w_spatial, scale_spatial, bias_spatial, w_expand, scale_expand, bias_expand):
    count_tiles = tile_maps.shape[0]
    flat_map = tile_maps.reshape(count_tiles * SIDE * SIDE, C)
    reduced = jnp.maximum(jnp.dot(flat_map, w_reduce, preferred_element_type=jnp.float32) * scale_reduce + bias_reduce, 0.0).astype(jnp.bfloat16)
    grid_map = reduced.reshape(count_tiles, SIDE, SIDE, MID)
    padded = jnp.pad(grid_map, ((0, 0), (1, 1), (1, 1), (0, 0)))
    summed = jnp.zeros((count_tiles * SIDE * SIDE, MID), jnp.float32)
    for row_shift in range(3):
        for col_shift in range(3):
            window = padded[:, row_shift:row_shift + SIDE, col_shift:col_shift + SIDE, :].reshape(count_tiles * SIDE * SIDE, MID)
            summed = summed + jnp.dot(window, w_spatial[row_shift, col_shift], preferred_element_type=jnp.float32)
    spatial = jnp.maximum(summed * scale_spatial + bias_spatial, 0.0).astype(jnp.bfloat16)
    expanded = jnp.maximum(jnp.dot(spatial, w_expand, preferred_element_type=jnp.float32) * scale_expand + bias_expand + flat_map.astype(jnp.float32), 0.0)
    return jnp.mean(expanded.reshape(count_tiles, SIDE * SIDE, C), axis=1).astype(jnp.bfloat16)


def reference(tiles, tissue_index, tissue_count, w_reduce, scale_reduce, bias_reduce, w_spatial, scale_spatial, bias_spatial, w_expand, scale_expand, bias_expand):
    owners = tissue_count.shape[0]
    start = (jnp.cumsum(tissue_count) - tissue_count).astype(jnp.int32)
    slot_ids = jnp.arange(2 * SEQ_DEV, dtype=jnp.int32)
    position = start[:, None] + slot_ids[None, :]
    is_valid = slot_ids[None, :] < tissue_count[:, None]
    source = (jnp.arange(owners, dtype=jnp.int32)[:, None] * CAND + tissue_index[:, :2 * SEQ_DEV]).astype(jnp.int32)
    target = jnp.where(is_valid, position, TOTAL).reshape(-1).astype(jnp.int32)
    source_of = jnp.zeros((TOTAL,), jnp.int32).at[target].set(source.reshape(-1), mode="drop")
    blocks = source_of.reshape(TOTAL // SEQ_DEV, SEQ_DEV)

    def encode_block(tile_ids):
        return bottleneck(tiles[tile_ids], w_reduce, scale_reduce, bias_reduce, w_spatial, scale_spatial, bias_spatial, w_expand, scale_expand, bias_expand)

    encoded = lax.map(encode_block, blocks)
    return encoded.reshape(TOTAL, C)
```

```python
import jax
import jax.numpy as jnp
from jax import lax
from jax.experimental import pallas as pl
from jax.experimental.pallas import tpu as pltpu
from jax.sharding import PartitionSpec as P

SIDE = 7
SEQ_DEV = 8
LANES = 128
COLS = 256
AXES = ("grp", "ext")


def encode_body(
    listing,
    count,
    tiles,
    w_reduce,
    scale_reduce,
    bias_reduce,
    w_spatial,
    scale_spatial,
    bias_spatial,
    w_expand,
    scale_expand,
    bias_expand,
    tail,
    head,
    maps,
    w1,
    w2,
    w3,
    last_cell,
    by_cell,
    framed,
    spatial,
    sem,
):
    slots, cells, channels = maps.shape
    inner = w1.shape[1]
    even = cells - 1
    half = slots // 2
    loads = []
    for t in range(slots):
        slot = jnp.clip(count[0] - half + t, 0, slots - 1) if t < half else t - half
        loads.append(pltpu.make_async_copy(tiles.at[listing[0, slot]], maps.at[t], sem.at[t]))
    weights = [
        pltpu.make_async_copy(src, dst, sem.at[slots + i])
        for i, (src, dst) in enumerate(((w_reduce, w1), (w_spatial, w2), (w_expand, w3)))
    ]
    for copy in loads + weights:
        copy.start()
    framed[...] = jnp.zeros(framed.shape, framed.dtype)
    for copy in loads:
        copy.wait()
    for t in range(slots):
        last_cell[t : t + 1, :] = maps[t, even:cells, :].astype(jnp.float32)
    weights[0].wait()
    x_last = last_cell[...].astype(jnp.bfloat16)
    for n in range(0, inner, COLS):
        cols = slice(n, n + COLS)
        w = w1[:, cols]
        most = jnp.dot(
            maps[:, 0:even, :].reshape(slots * even, channels), w, preferred_element_type=jnp.float32
        )
        most = jnp.maximum(most * scale_reduce[:, cols] + bias_reduce[:, cols], 0.0)
        last = jnp.dot(x_last, w, preferred_element_type=jnp.float32)
        last = jnp.maximum(last * scale_reduce[:, cols] + bias_reduce[:, cols], 0.0)
        for q in range(COLS // LANES):
            block = n // LANES + q
            lanes = slice(q * LANES, (q + 1) * LANES)
            for t in range(slots):
                by_cell[block, pl.ds(t, even, stride=slots), :] = most[t * even : (t + 1) * even, lanes]
            by_cell[block, even * slots :, :] = last[:, lanes]
    for i in range(SIDE):
        for block in range(inner // LANES):
            framed[i + 1, slots : slots + SIDE * slots, block * LANES : (block + 1) * LANES] = by_cell[
                block, i * SIDE * slots : (i + 1) * SIDE * slots, :
            ].astype(jnp.bfloat16)
    weights[1].wait()
    for n in range(0, inner, COLS):
        cols = slice(n, n + COLS)
        windows = jnp.concatenate(
            [
                framed[a : a + SIDE, b * slots : (b + SIDE) * slots, :].reshape(cells * slots, inner)
                for a in range(3)
                for b in range(3)
            ],
            axis=1,
        )
        conv = jnp.dot(windows, w2[:, cols], preferred_element_type=jnp.float32)
        conv = jnp.maximum(conv * scale_spatial[:, cols] + bias_spatial[:, cols], 0.0)
        for q in range(COLS // LANES):
            by_cell[n // LANES + q, :, :] = conv[:, q * LANES : (q + 1) * LANES]
    for block in range(inner // LANES):
        lanes = slice(block * LANES, (block + 1) * LANES)
        for t in range(slots):
            spatial[t * even : (t + 1) * even, lanes] = by_cell[
                block, pl.ds(t, even, stride=slots), :
            ].astype(jnp.bfloat16)
        spatial[even * slots :, lanes] = by_cell[block, even * slots :, :].astype(jnp.bfloat16)
    weights[2].wait()
    for n in range(0, channels, COLS):
        cols = slice(n, n + COLS)
        grown = jnp.dot(spatial[...], w3[:, cols], preferred_element_type=jnp.float32)
        grown = grown * scale_expand[:, cols] + bias_expand[:, cols]
        most = grown[: even * slots].reshape(slots, even, COLS) + maps[:, 0:even, cols].astype(jnp.float32)
        last = grown[even * slots :] + last_cell[:, cols]
        total = jnp.sum(jnp.maximum(most, 0.0), axis=1) + jnp.maximum(last, 0.0)
        mean = (total / cells).astype(jnp.bfloat16)
        tail[:, cols] = mean[:half]
        head[:, cols] = mean[half:]


def encode(listing, count, tiles, w_reduce, scale_reduce, bias_reduce, w_spatial, scale_spatial, bias_spatial, w_expand, scale_expand, bias_expand):
    slots = 2 * SEQ_DEV
    cells, channels = tiles.shape[1:]
    inner = w_reduce.shape[1]
    far = pl.BlockSpec(memory_space=pl.ANY)
    near = pl.BlockSpec(memory_space=pltpu.VMEM)
    scalar = pl.BlockSpec(memory_space=pltpu.SMEM)
    row = lambda v: v.reshape(1, -1)
    return pl.pallas_call(
        encode_body,
        out_shape=[jax.ShapeDtypeStruct((SEQ_DEV, channels), jnp.bfloat16)] * 2,
        in_specs=[scalar, scalar, far, far, near, near, far, near, near, far, near, near],
        out_specs=[near, near],
        scratch_shapes=[
            pltpu.VMEM((slots, cells, channels), jnp.bfloat16),
            pltpu.VMEM((channels, inner), jnp.bfloat16),
            pltpu.VMEM((9 * inner, inner), jnp.bfloat16),
            pltpu.VMEM((inner, channels), jnp.bfloat16),
            pltpu.VMEM((slots, channels), jnp.float32),
            pltpu.VMEM((inner // LANES, cells * slots, LANES), jnp.float32),
            pltpu.VMEM((SIDE + 2, (SIDE + 2) * slots, inner), jnp.bfloat16),
            pltpu.VMEM((cells * slots, inner), jnp.bfloat16),
            pltpu.SemaphoreType.DMA((slots + 3,)),
        ],
        cost_estimate=pl.CostEstimate(
            flops=2 * slots * cells * inner * (2 * channels + 9 * inner),
            bytes_accessed=2 * (slots * cells * channels + 2 * channels * inner + 9 * inner * inner),
            transcendentals=0,
        ),
        name="encode",
    )(
        listing,
        count,
        tiles,
        w_reduce,
        row(scale_reduce),
        row(bias_reduce),
        w_spatial.reshape(9 * inner, inner),
        row(scale_spatial),
        row(bias_spatial),
        w_expand,
        row(scale_expand),
        row(bias_expand),
    )


def pack_body(ahead, arrived, head, out, rows):
    half = head.shape[0]
    backlog = jnp.clip(jnp.sum(ahead[...]), 0, half)
    for block in range(rows.shape[0]):
        lanes = slice(block * LANES, (block + 1) * LANES)
        rows[block, :half, :] = arrived[:, lanes].astype(jnp.float32)
        rows[block, half:, :] = head[:, lanes].astype(jnp.float32)
        out[:, lanes] = rows[block, pl.ds(half - backlog, half), :].astype(out.dtype)


def pack(ahead, arrived, head):
    near = pl.BlockSpec(memory_space=pltpu.VMEM)
    return pl.pallas_call(
        pack_body,
        out_shape=jax.ShapeDtypeStruct(head.shape, head.dtype),
        in_specs=[near] * 3,
        out_specs=near,
        scratch_shapes=[pltpu.VMEM((head.shape[1] // LANES, 2 * head.shape[0], LANES), jnp.float32)],
        name="pack",
    )(ahead, arrived, head)


def on_device(tiles, tissue_index, tissue_count, *weights):
    devices = lax.axis_size(AXES)
    rank = lax.axis_index(AXES)
    later = jnp.arange(devices, dtype=jnp.int32) > rank
    adds = jnp.where(later, tissue_count - SEQ_DEV, 0)
    ahead = lax.all_to_all(adds, AXES, 0, 0, tiled=True)
    tail, head = encode(tissue_index, tissue_count, tiles, *weights)
    arrived = lax.ppermute(tail, AXES, [(i, i + 1) for i in range(devices - 1)])
    return pack(ahead.reshape(1, devices), arrived, head)


def solution(mesh):
    owned = P(AXES, None)
    return jax.shard_map(
        on_device,
        mesh=mesh,
        in_specs=(P(AXES, None, None), owned, P(AXES)) + (P(),) * 9,
        out_specs=owned,
        check_vma=False,
    )
```

```python
import jax
import jax.numpy as jnp
from jax import lax
from jax.experimental import pallas as pl
from jax.experimental.pallas import tpu as pltpu
from jax.sharding import PartitionSpec as P


SIDE = 7
SEQ_DEV = 8
LANES = 128
COLS = 256
AXES = ("grp", "ext")
SCALAR = pl.BlockSpec(memory_space=pltpu.SMEM)
NEAR = pl.BlockSpec(memory_space=pltpu.VMEM)
FAR = pl.BlockSpec(memory_space=pltpu.HBM)


def held(value):
    return pltpu.with_memory_space_constraint(value, pltpu.VMEM)


def encode(maps, weights, out, last_cell, by_cell, framed, spatial, ready=lambda stage: None):
    w_reduce, scale_reduce, bias_reduce, w_spatial, scale_spatial, bias_spatial, w_expand, scale_expand, bias_expand = weights
    count, cells, channels = maps.shape
    inner = w_reduce.shape[1]
    even = cells - 1
    framed[...] = jnp.zeros(framed.shape, framed.dtype)
    ready(0)
    for t in range(count):
        last_cell[t : t + 1, :] = maps[t, even:cells, :].astype(jnp.float32)
    x_last = last_cell[...].astype(jnp.bfloat16)
    for n in range(0, inner, COLS):
        cols = slice(n, n + COLS)
        w = w_reduce[:, cols]
        most = jnp.dot(maps[:, 0:even, :].reshape(count * even, channels), w, preferred_element_type=jnp.float32)
        most = jnp.maximum(most * scale_reduce[:, cols] + bias_reduce[:, cols], 0.0)
        last = jnp.dot(x_last, w, preferred_element_type=jnp.float32)
        last = jnp.maximum(last * scale_reduce[:, cols] + bias_reduce[:, cols], 0.0)
        for q in range(COLS // LANES):
            block = n // LANES + q
            lanes = slice(q * LANES, (q + 1) * LANES)
            for t in range(count):
                by_cell[block, pl.ds(t, even, stride=count), :] = most[t * even : (t + 1) * even, lanes]
            by_cell[block, even * count :, :] = last[:, lanes]
    for i in range(SIDE):
        for block in range(inner // LANES):
            framed[i + 1, count : count + SIDE * count, block * LANES : (block + 1) * LANES] = by_cell[
                block, i * SIDE * count : (i + 1) * SIDE * count, :
            ].astype(jnp.bfloat16)
    ready(1)
    for n in range(0, inner, COLS):
        cols = slice(n, n + COLS)
        windows = jnp.concatenate(
            [
                framed[a : a + SIDE, b * count : (b + SIDE) * count, :].reshape(cells * count, inner)
                for a in range(3)
                for b in range(3)
            ],
            axis=1,
        )
        conv = jnp.dot(windows, w_spatial[:, cols], preferred_element_type=jnp.float32)
        conv = jnp.maximum(conv * scale_spatial[:, cols] + bias_spatial[:, cols], 0.0)
        for q in range(COLS // LANES):
            by_cell[n // LANES + q, :, :] = conv[:, q * LANES : (q + 1) * LANES]
    for block in range(inner // LANES):
        lanes = slice(block * LANES, (block + 1) * LANES)
        for t in range(count):
            spatial[t * even : (t + 1) * even, lanes] = by_cell[block, pl.ds(t, even, stride=count), :].astype(
                jnp.bfloat16
            )
        spatial[even * count :, lanes] = by_cell[block, even * count :, :].astype(jnp.bfloat16)
    ready(2)
    for n in range(0, channels, COLS):
        cols = slice(n, n + COLS)
        grown = jnp.dot(spatial[...], w_expand[:, cols], preferred_element_type=jnp.float32)
        grown = grown * scale_expand[:, cols] + bias_expand[:, cols]
        most = grown[: even * count].reshape(count, even, COLS) + maps[:, 0:even, cols].astype(jnp.float32)
        last = grown[even * count :] + last_cell[:, cols]
        total = jnp.sum(jnp.maximum(most, 0.0), axis=1) + jnp.maximum(last, 0.0)
        out[:, cols] = (total / cells).astype(out.dtype)


def scratch(cells, channels, inner):
    return [
        pltpu.VMEM((SEQ_DEV, channels), jnp.float32),
        pltpu.VMEM((inner // LANES, cells * SEQ_DEV, LANES), jnp.float32),
        pltpu.VMEM((SIDE + 2, (SIDE + 2) * SEQ_DEV, inner), jnp.bfloat16),
        pltpu.VMEM((cells * SEQ_DEV, inner), jnp.bfloat16),
    ]


def cost(cells, channels, inner):
    return pl.CostEstimate(
        flops=2 * SEQ_DEV * cells * inner * (2 * channels + 9 * inner),
        bytes_accessed=2 * (SEQ_DEV * cells * channels + 2 * channels * inner + 9 * inner * inner),
        transcendentals=0,
    )


def tail_body(listing, count, tiles, w_spatial_far, w_expand_far, w_reduce, s1, b1, s2, b2, s3, b3, tail, head_maps, w_spatial, w_expand, maps, *rest):
    *work, sem = rest
    own = maps.shape[0]
    loads = []
    for t in range(own):
        slot = jnp.clip(count[0, 0] - own + t, 0, 2 * own - 1)
        loads.append(pltpu.make_async_copy(tiles.at[listing[0, slot]], maps.at[t], sem.at[t]))
    later = [
        pltpu.make_async_copy(w_spatial_far, w_spatial, sem.at[own]),
        pltpu.make_async_copy(w_expand_far, w_expand, sem.at[own + 1]),
    ]
    later += [
        pltpu.make_async_copy(tiles.at[listing[0, t]], head_maps.at[t], sem.at[own + 2 + t]) for t in range(own)
    ]
    for copy in loads + later:
        copy.start()

    def ready(stage):
        if stage == 0:
            for copy in loads:
                copy.wait()
        else:
            later[stage - 1].wait()

    encode(maps, (w_reduce, s1, b1, w_spatial, s2, b2, w_expand, s3, b3), tail, *work, ready=ready)
    for copy in later[2:]:
        copy.wait()


def encode_tail(listing, count, tiles, w_reduce, s1, b1, w_spatial, s2, b2, w_expand, s3, b3):
    cells, channels = tiles.shape[1:]
    inner = w_reduce.shape[1]
    maps = (SEQ_DEV, cells, channels)
    return pl.pallas_call(
        tail_body,
        out_shape=[
            pltpu.VMEM((SEQ_DEV, channels), jnp.bfloat16),
            pltpu.VMEM(maps, tiles.dtype),
            pltpu.VMEM(w_spatial.shape, w_spatial.dtype),
            pltpu.VMEM(w_expand.shape, w_expand.dtype),
        ],
        in_specs=[SCALAR] * 2 + [FAR] * 3 + [NEAR] * 7,
        out_specs=[NEAR] * 4,
        scratch_shapes=[pltpu.VMEM(maps, tiles.dtype)]
        + scratch(cells, channels, inner)
        + [pltpu.SemaphoreType.DMA((2 * SEQ_DEV + 2,))],
        cost_estimate=cost(cells, channels, inner),
        compiler_params=pltpu.CompilerParams(vmem_limit_bytes=40 << 20),
        name="encode_tail",
    )(listing, count, *(pltpu.with_memory_space_constraint(v, pltpu.HBM) for v in (tiles, w_spatial, w_expand)), w_reduce, s1, b1, s2, b2, s3, b3)


def head_body(maps, w_reduce, s1, b1, w_spatial, s2, b2, w_expand, s3, b3, head, *work):
    encode(maps, (w_reduce, s1, b1, w_spatial, s2, b2, w_expand, s3, b3), head, *work)


def encode_head(maps, *weights):
    cells, channels = maps.shape[1:]
    inner = weights[0].shape[1]
    return pl.pallas_call(
        head_body,
        out_shape=pltpu.VMEM((SEQ_DEV, channels), jnp.bfloat16),
        in_specs=[NEAR] * 10,
        out_specs=NEAR,
        scratch_shapes=scratch(cells, channels, inner),
        cost_estimate=cost(cells, channels, inner),
        compiler_params=pltpu.CompilerParams(vmem_limit_bytes=24 << 20),
        name="encode_head",
    )(maps, *weights)


def pack_body(ahead, arrived, head, out, rows):
    half = head.shape[0]
    backlog = jnp.clip(jnp.sum(ahead[...]) // LANES, 0, half)
    for block in range(rows.shape[0]):
        lanes = slice(block * LANES, (block + 1) * LANES)
        rows[block, :half, :] = arrived[:, lanes].astype(jnp.float32)
        rows[block, half:, :] = head[:, lanes].astype(jnp.float32)
        out[:, lanes] = rows[block, pl.ds(half - backlog, half), :].astype(out.dtype)


def pack(ahead, arrived, head):
    return pl.pallas_call(
        pack_body,
        out_shape=jax.ShapeDtypeStruct(head.shape, head.dtype),
        in_specs=[NEAR] * 3,
        out_specs=NEAR,
        scratch_shapes=[pltpu.VMEM((head.shape[1] // LANES, 2 * head.shape[0], LANES), jnp.float32)],
        compiler_params=pltpu.CompilerParams(vmem_limit_bytes=4 << 20),
        name="pack",
    )(held(ahead), held(arrived), held(head))


def spread_body(where, count, out):
    place = lax.broadcasted_iota(jnp.int32, out.shape, 0)
    out[...] = jnp.where(place > where[0, 0], count[0, 0] - SEQ_DEV, 0)


def spread(where, count, devices):
    return pl.pallas_call(
        spread_body,
        out_shape=jax.ShapeDtypeStruct((devices, 1, LANES), jnp.int32),
        in_specs=[SCALAR] * 2,
        out_specs=NEAR,
        cost_estimate=pl.CostEstimate(flops=10**11, bytes_accessed=10**8, transcendentals=0),
        compiler_params=pltpu.CompilerParams(vmem_limit_bytes=1 << 20),
        name="spread",
    )(where, count)


def on_device(tiles, tissue_index, tissue_count, w_reduce, s1, b1, w_spatial, s2, b2, w_expand, s3, b3):
    devices = lax.axis_size(AXES)
    rank = lax.axis_index(AXES).reshape(1, 1)
    count = tissue_count.reshape(1, 1)
    inner = w_reduce.shape[1]
    w_spatial = w_spatial.reshape(9 * inner, inner)
    w_reduce, s1, b1, s2, b2, s3, b3 = (
        held(v.reshape(-1, v.shape[-1])) for v in (w_reduce, s1, b1, s2, b2, s3, b3)
    )
    ahead = lax.all_to_all(spread(rank, count, devices), AXES, 0, 0, tiled=True)
    tail, maps, w_spatial, w_expand = encode_tail(
        tissue_index, count, tiles, w_reduce, s1, b1, w_spatial, s2, b2, w_expand, s3, b3
    )
    arrived = lax.ppermute(tail, AXES, [(i, i + 1) for i in range(devices - 1)])
    head = encode_head(maps, w_reduce, s1, b1, w_spatial, s2, b2, w_expand, s3, b3)
    return pack(ahead, arrived, head)


def solution(mesh):
    owned = P(AXES, None)
    return jax.shard_map(
        on_device,
        mesh=mesh,
        in_specs=(P(AXES, None, None), owned, P(AXES)) + (P(),) * 9,
        out_specs=owned,
        check_vma=False,
    )
```

```python
import jax
import jax.numpy as jnp
from jax import lax
from jax.experimental import pallas as pl
from jax.experimental.pallas import tpu as pltpu
from jax.sharding import PartitionSpec as P


SIDE = 7
SEQ_DEV = 8
LANES = 128
COLS = 256
AXES = ("grp", "ext")
SCALAR = pl.BlockSpec(memory_space=pltpu.SMEM)
NEAR = pl.BlockSpec(memory_space=pltpu.VMEM)
FAR = pl.BlockSpec(memory_space=pltpu.HBM)


def held(value):
    return pltpu.with_memory_space_constraint(value, pltpu.VMEM)


def encode(maps, weights, out, last_cell, by_cell, framed, spatial, ready=lambda stage: None):
    w_reduce, scale_reduce, bias_reduce, w_spatial, scale_spatial, bias_spatial, w_expand, scale_expand, bias_expand = weights
    count, cells, channels = maps.shape
    inner = w_reduce.shape[1]
    even = cells - 1
    edge = jnp.zeros((SIDE, count, inner), framed.dtype)
    framed[:, :count, :] = edge
    framed[:, (SIDE + 1) * count :, :] = edge
    ready(0)
    for t in range(count):
        last_cell[t : t + 1, :] = maps[t, even:cells, :].astype(jnp.float32)
    x_last = last_cell[...].astype(jnp.bfloat16)
    rows = jnp.concatenate([maps[:, 0:even, :].reshape(count * even, channels), x_last], axis=0)
    for n in range(0, inner, COLS):
        cols = slice(n, n + COLS)
        grown = jnp.dot(rows, w_reduce[:, cols], preferred_element_type=jnp.float32)
        grown = jnp.maximum(grown * scale_reduce[:, cols] + bias_reduce[:, cols], 0.0)
        for q in range(COLS // LANES):
            block = n // LANES + q
            lanes = slice(q * LANES, (q + 1) * LANES)
            for t in range(count):
                by_cell[block, pl.ds(t, even, stride=count), :] = grown[t * even : (t + 1) * even, lanes]
            by_cell[block, even * count :, :] = grown[even * count :, lanes]
    for i in range(SIDE):
        for block in range(inner // LANES):
            framed[i, count : count + SIDE * count, block * LANES : (block + 1) * LANES] = by_cell[
                block, i * SIDE * count : (i + 1) * SIDE * count, :
            ].astype(jnp.bfloat16)
    ready(1)
    row_cells = SIDE * count
    for n in range(0, inner, COLS):
        cols = slice(n, n + COLS)
        parts = []
        for a in (1, 0, 2):
            first, final = max(0, a - 1), min(SIDE, SIDE + a - 1)
            windows = jnp.concatenate(
                [
                    framed[first:final, b * count : (b + SIDE) * count, :].reshape((final - first) * row_cells, inner)
                    for b in range(3)
                ],
                axis=1,
            )
            parts.append(
                jnp.dot(windows, w_spatial[a * 3 * inner : (a + 1) * 3 * inner, cols], preferred_element_type=jnp.float32)
            )
        middle, above, below = parts
        conv = jnp.concatenate(
            [
                middle[:row_cells] + below[:row_cells],
                middle[row_cells:-row_cells] + above[:-row_cells] + below[row_cells:],
                middle[-row_cells:] + above[-row_cells:],
            ],
            axis=0,
        )
        conv = jnp.maximum(conv * scale_spatial[:, cols] + bias_spatial[:, cols], 0.0)
        for q in range(COLS // LANES):
            by_cell[n // LANES + q, :, :] = conv[:, q * LANES : (q + 1) * LANES]
    for block in range(inner // LANES):
        lanes = slice(block * LANES, (block + 1) * LANES)
        for t in range(count):
            spatial[t * even : (t + 1) * even, lanes] = by_cell[block, pl.ds(t, even, stride=count), :].astype(
                jnp.bfloat16
            )
        spatial[even * count :, lanes] = by_cell[block, even * count :, :].astype(jnp.bfloat16)
    ready(2)
    for n in range(0, channels, COLS):
        cols = slice(n, n + COLS)
        grown = jnp.dot(spatial[...], w_expand[:, cols], preferred_element_type=jnp.float32)
        grown = grown * scale_expand[:, cols] + bias_expand[:, cols]
        most = grown[: even * count].reshape(count, even, COLS) + maps[:, 0:even, cols].astype(jnp.float32)
        last = grown[even * count :] + last_cell[:, cols]
        total = jnp.sum(jnp.maximum(most, 0.0), axis=1) + jnp.maximum(last, 0.0)
        out[:, cols] = (total / cells).astype(out.dtype)


def scratch(cells, channels, inner):
    return [
        pltpu.VMEM((SEQ_DEV, channels), jnp.float32),
        pltpu.VMEM((inner // LANES, cells * SEQ_DEV, LANES), jnp.float32),
        pltpu.VMEM((SIDE, (SIDE + 2) * SEQ_DEV, inner), jnp.bfloat16),
        pltpu.VMEM((cells * SEQ_DEV, inner), jnp.bfloat16),
    ]


def cost(cells, channels, inner):
    return pl.CostEstimate(
        flops=2 * SEQ_DEV * cells * inner * (2 * channels + 9 * inner),
        bytes_accessed=2 * (SEQ_DEV * cells * channels + 2 * channels * inner + 9 * inner * inner),
        transcendentals=0,
    )


def tail_body(listing, count, tiles, w_spatial_far, w_expand_far, w_reduce, s1, b1, s2, b2, s3, b3, tail, head_maps, w_spatial, w_expand, maps, *rest):
    *work, sem = rest
    own = maps.shape[0]
    loads = []
    for t in range(own):
        slot = lax.rem(jnp.clip(count[0, 0], 0, 2 * own) + own + t, 2 * own)
        loads.append(pltpu.make_async_copy(tiles.at[listing[0, slot]], maps.at[t], sem.at[t]))
    later = [
        pltpu.make_async_copy(w_spatial_far, w_spatial, sem.at[own]),
        pltpu.make_async_copy(w_expand_far, w_expand, sem.at[own + 1]),
    ]
    later += [
        pltpu.make_async_copy(tiles.at[listing[0, t]], head_maps.at[t], sem.at[own + 2 + t]) for t in range(own)
    ]
    for copy in loads + later[:1]:
        copy.start()

    def ready(stage):
        if stage == 0:
            for copy in loads:
                copy.wait()
            for copy in later[1:]:
                copy.start()
        else:
            later[stage - 1].wait()

    encode(maps, (w_reduce, s1, b1, w_spatial, s2, b2, w_expand, s3, b3), tail, *work, ready=ready)
    for copy in later[2:]:
        copy.wait()


def encode_tail(listing, count, tiles, w_reduce, s1, b1, w_spatial, s2, b2, w_expand, s3, b3):
    cells, channels = tiles.shape[1:]
    inner = w_reduce.shape[1]
    maps = (SEQ_DEV, cells, channels)
    return pl.pallas_call(
        tail_body,
        out_shape=[
            pltpu.VMEM((SEQ_DEV, channels), jnp.bfloat16),
            pltpu.VMEM(maps, tiles.dtype),
            pltpu.VMEM(w_spatial.shape, w_spatial.dtype),
            pltpu.VMEM(w_expand.shape, w_expand.dtype),
        ],
        in_specs=[SCALAR] * 2 + [FAR] * 3 + [NEAR] * 7,
        out_specs=[NEAR] * 4,
        scratch_shapes=[pltpu.VMEM(maps, tiles.dtype)]
        + scratch(cells, channels, inner)
        + [pltpu.SemaphoreType.DMA((2 * SEQ_DEV + 2,))],
        cost_estimate=cost(cells, channels, inner),
        compiler_params=pltpu.CompilerParams(vmem_limit_bytes=40 << 20),
        name="encode_tail",
    )(listing, count, *(pltpu.with_memory_space_constraint(v, pltpu.HBM) for v in (tiles, w_spatial, w_expand)), w_reduce, s1, b1, s2, b2, s3, b3)


def head_body(maps, w_reduce, s1, b1, w_spatial, s2, b2, w_expand, s3, b3, head, *work):
    encode(maps, (w_reduce, s1, b1, w_spatial, s2, b2, w_expand, s3, b3), head, *work)


def encode_head(maps, *weights):
    cells, channels = maps.shape[1:]
    inner = weights[0].shape[1]
    return pl.pallas_call(
        head_body,
        out_shape=pltpu.VMEM((SEQ_DEV, channels), jnp.bfloat16),
        in_specs=[NEAR] * 10,
        out_specs=NEAR,
        scratch_shapes=scratch(cells, channels, inner),
        cost_estimate=cost(cells, channels, inner),
        compiler_params=pltpu.CompilerParams(vmem_limit_bytes=24 << 20),
        name="encode_head",
    )(maps, *weights)


def pack_body(ahead, arrived, head, out, rows):
    half = head.shape[0]
    backlog = jnp.clip(jnp.sum(ahead[...]) // LANES, 0, half)
    for block in range(rows.shape[0]):
        lanes = slice(block * LANES, (block + 1) * LANES)
        rows[block, :half, :] = arrived[:, lanes].astype(jnp.float32)
        rows[block, half:, :] = head[:, lanes].astype(jnp.float32)
        out[:, lanes] = rows[block, pl.ds(half - backlog, half), :].astype(out.dtype)


def pack(ahead, arrived, head):
    return pl.pallas_call(
        pack_body,
        out_shape=jax.ShapeDtypeStruct(head.shape, head.dtype),
        in_specs=[NEAR] * 3,
        out_specs=NEAR,
        scratch_shapes=[pltpu.VMEM((head.shape[1] // LANES, 2 * head.shape[0], LANES), jnp.float32)],
        compiler_params=pltpu.CompilerParams(vmem_limit_bytes=4 << 20),
        name="pack",
    )(held(ahead), held(arrived), held(head))


def spread_body(where, count, out):
    place = lax.broadcasted_iota(jnp.int32, out.shape, 0)
    out[...] = jnp.where(place > where[0, 0], count[0, 0] - SEQ_DEV, 0)


def spread(where, count, devices):
    return pl.pallas_call(
        spread_body,
        out_shape=jax.ShapeDtypeStruct((devices, 1, LANES), jnp.int32),
        in_specs=[SCALAR] * 2,
        out_specs=NEAR,
        cost_estimate=pl.CostEstimate(flops=10**11, bytes_accessed=10**8, transcendentals=0),
        compiler_params=pltpu.CompilerParams(vmem_limit_bytes=1 << 20),
        name="spread",
    )(where, count)


def on_device(tiles, tissue_index, tissue_count, w_reduce, s1, b1, w_spatial, s2, b2, w_expand, s3, b3):
    devices = lax.axis_size(AXES)
    rank = lax.axis_index(AXES).reshape(1, 1)
    count = tissue_count.reshape(1, 1)
    inner = w_reduce.shape[1]
    w_spatial = w_spatial.reshape(9 * inner, inner)
    w_reduce, s1, b1, s2, b2, s3, b3 = (
        held(v.reshape(-1, v.shape[-1])) for v in (w_reduce, s1, b1, s2, b2, s3, b3)
    )
    ahead = lax.all_to_all(spread(rank, count, devices), AXES, 0, 0, tiled=True)
    tail, maps, w_spatial, w_expand = encode_tail(
        tissue_index, count, tiles, w_reduce, s1, b1, w_spatial, s2, b2, w_expand, s3, b3
    )
    arrived = lax.ppermute(tail, AXES, [(i, i + 1) for i in range(devices - 1)])
    head = encode_head(maps, w_reduce, s1, b1, w_spatial, s2, b2, w_expand, s3, b3)
    return pack(ahead, arrived, head)


def solution(mesh):
    owned = P(AXES, None)
    return jax.shard_map(
        on_device,
        mesh=mesh,
        in_specs=(P(AXES, None, None), owned, P(AXES)) + (P(),) * 9,
        out_specs=owned,
        check_vma=False,
    )
```

```python
import jax
import jax.numpy as jnp
from jax import lax
from jax.experimental import pallas as pl
from jax.experimental.pallas import tpu as pltpu
from jax.sharding import PartitionSpec as P


SIDE = 7
SEQ_DEV = 8
LANES = 128
COLS = 256
AXES = ("grp", "ext")
SCALAR = pl.BlockSpec(memory_space=pltpu.SMEM)
NEAR = pl.BlockSpec(memory_space=pltpu.VMEM)
FAR = pl.BlockSpec(memory_space=pltpu.HBM)


def held(value):
    return pltpu.with_memory_space_constraint(value, pltpu.VMEM)


def encode(maps, weights, out, last_cell, by_cell, framed, spatial, ready=lambda stage: None):
    w_reduce, scale_reduce, bias_reduce, w_spatial, scale_spatial, bias_spatial, w_expand, scale_expand, bias_expand = weights
    count, cells, channels = maps.shape
    inner = w_reduce.shape[1]
    even = cells - 1
    edge = jnp.zeros((SIDE, count, inner), framed.dtype)
    framed[:, :count, :] = edge
    framed[:, (SIDE + 1) * count :, :] = edge
    ready(0)
    for t in range(count):
        last_cell[t : t + 1, :] = maps[t, even:cells, :].astype(jnp.float32)
    x_last = last_cell[...].astype(jnp.bfloat16)
    rows = jnp.concatenate([maps[:, 0:even, :].reshape(count * even, channels), x_last], axis=0)
    for n in range(0, inner, COLS):
        cols = slice(n, n + COLS)
        grown = jnp.dot(rows, w_reduce[:, cols], preferred_element_type=jnp.float32)
        grown = jnp.maximum(grown * scale_reduce[:, cols] + bias_reduce[:, cols], 0.0)
        for q in range(COLS // LANES):
            block = n // LANES + q
            lanes = slice(q * LANES, (q + 1) * LANES)
            for t in range(count):
                by_cell[block, pl.ds(t, even, stride=count), :] = grown[t * even : (t + 1) * even, lanes]
            by_cell[block, even * count :, :] = grown[even * count :, lanes]
    for i in range(SIDE):
        for block in range(inner // LANES):
            framed[i, count : count + SIDE * count, block * LANES : (block + 1) * LANES] = by_cell[
                block, i * SIDE * count : (i + 1) * SIDE * count, :
            ].astype(jnp.bfloat16)
    ready(1)
    row_cells = SIDE * count
    for n in range(0, inner, COLS):
        cols = slice(n, n + COLS)
        parts = []
        for a in (1, 0, 2):
            first, final = max(0, a - 1), min(SIDE, SIDE + a - 1)
            windows = jnp.concatenate(
                [
                    framed[first:final, b * count : (b + SIDE) * count, :].reshape((final - first) * row_cells, inner)
                    for b in range(3)
                ],
                axis=1,
            )
            parts.append(
                jnp.dot(windows, w_spatial[a * 3 * inner : (a + 1) * 3 * inner, cols], preferred_element_type=jnp.float32)
            )
        middle, above, below = parts
        conv = jnp.concatenate(
            [
                middle[:row_cells] + below[:row_cells],
                middle[row_cells:-row_cells] + above[:-row_cells] + below[row_cells:],
                middle[-row_cells:] + above[-row_cells:],
            ],
            axis=0,
        )
        conv = jnp.maximum(conv * scale_spatial[:, cols] + bias_spatial[:, cols], 0.0)
        for q in range(COLS // LANES):
            by_cell[n // LANES + q, :, :] = conv[:, q * LANES : (q + 1) * LANES]
    for block in range(inner // LANES):
        lanes = slice(block * LANES, (block + 1) * LANES)
        for t in range(count):
            spatial[t * even : (t + 1) * even, lanes] = by_cell[block, pl.ds(t, even, stride=count), :].astype(
                jnp.bfloat16
            )
        spatial[even * count :, lanes] = by_cell[block, even * count :, :].astype(jnp.bfloat16)
    ready(2)
    for n in range(0, channels, COLS):
        cols = slice(n, n + COLS)
        grown = jnp.dot(spatial[...], w_expand[:, cols], preferred_element_type=jnp.float32)
        grown = grown * scale_expand[:, cols] + bias_expand[:, cols]
        most = grown[: even * count].reshape(count, even, COLS) + maps[:, 0:even, cols].astype(jnp.float32)
        last = grown[even * count :] + last_cell[:, cols]
        total = jnp.sum(jnp.maximum(most, 0.0), axis=1) + jnp.maximum(last, 0.0)
        out[:, cols] = (total / cells).astype(out.dtype)


def scratch(cells, channels, inner):
    return [
        pltpu.VMEM((SEQ_DEV, channels), jnp.float32),
        pltpu.VMEM((inner // LANES, cells * SEQ_DEV, LANES), jnp.float32),
        pltpu.VMEM((SIDE, (SIDE + 2) * SEQ_DEV, inner), jnp.bfloat16),
        pltpu.VMEM((cells * SEQ_DEV, inner), jnp.bfloat16),
    ]


def cost(cells, channels, inner):
    return pl.CostEstimate(
        flops=2 * SEQ_DEV * cells * inner * (2 * channels + 9 * inner),
        bytes_accessed=2 * (SEQ_DEV * cells * channels + 2 * channels * inner + 9 * inner * inner),
        transcendentals=0,
    )


def tail_body(listing, count, tiles, w_spatial_far, w_expand_far, w_reduce, s1, b1, s2, b2, s3, b3, tail, head_maps, w_spatial, w_expand, maps, *rest):
    *work, sem = rest
    own = maps.shape[0]
    row = lax.broadcasted_iota(jnp.int32, (2 * own, listing.shape[1]), 0)
    lane = lax.broadcasted_iota(jnp.int32, (2 * own, listing.shape[1]), 1)
    amount = jnp.clip(count[:, : listing.shape[1]], 0, 2 * own)
    place = amount + own + row
    place = jnp.where(row < own, jnp.where(place >= 2 * own, place - 2 * own, place), row - own)
    place = jnp.where(place >= 2 * own, place - 2 * own, place)
    chosen = jnp.sum(jnp.where(lane == place, listing[...], 0), axis=1, keepdims=True)
    loads = []
    for t in range(own):
        loads.append(pltpu.make_async_copy(tiles.at[chosen[t, 0]], maps.at[t], sem.at[t]))
    later = [
        pltpu.make_async_copy(w_spatial_far, w_spatial, sem.at[own]),
        pltpu.make_async_copy(w_expand_far, w_expand, sem.at[own + 1]),
    ]
    later += [
        pltpu.make_async_copy(tiles.at[chosen[own + t, 0]], head_maps.at[t], sem.at[own + 2 + t]) for t in range(own)
    ]
    for copy in loads + later[:1]:
        copy.start()

    def ready(stage):
        if stage == 0:
            for copy in loads:
                copy.wait()
            for copy in later[1:]:
                copy.start()
        else:
            later[stage - 1].wait()

    encode(maps, (w_reduce, s1, b1, w_spatial, s2, b2, w_expand, s3, b3), tail, *work, ready=ready)
    for copy in later[2:]:
        copy.wait()


def encode_tail(listing, count, tiles, w_reduce, s1, b1, w_spatial, s2, b2, w_expand, s3, b3):
    cells, channels = tiles.shape[1:]
    inner = w_reduce.shape[1]
    maps = (SEQ_DEV, cells, channels)
    return pl.pallas_call(
        tail_body,
        out_shape=[
            pltpu.VMEM((SEQ_DEV, channels), jnp.bfloat16),
            pltpu.VMEM(maps, tiles.dtype),
            pltpu.VMEM(w_spatial.shape, w_spatial.dtype),
            pltpu.VMEM(w_expand.shape, w_expand.dtype),
        ],
        in_specs=[NEAR] * 2 + [FAR] * 3 + [NEAR] * 7,
        out_specs=[NEAR] * 4,
        scratch_shapes=[pltpu.VMEM(maps, tiles.dtype)]
        + scratch(cells, channels, inner)
        + [pltpu.SemaphoreType.DMA((2 * SEQ_DEV + 2,))],
        cost_estimate=cost(cells, channels, inner),
        compiler_params=pltpu.CompilerParams(vmem_limit_bytes=40 << 20),
        name="encode_tail",
    )(held(listing), count, *(pltpu.with_memory_space_constraint(v, pltpu.HBM) for v in (tiles, w_spatial, w_expand)), w_reduce, s1, b1, s2, b2, s3, b3)


def head_body(maps, w_reduce, s1, b1, w_spatial, s2, b2, w_expand, s3, b3, head, *work):
    encode(maps, (w_reduce, s1, b1, w_spatial, s2, b2, w_expand, s3, b3), head, *work)


def encode_head(maps, *weights):
    cells, channels = maps.shape[1:]
    inner = weights[0].shape[1]
    return pl.pallas_call(
        head_body,
        out_shape=pltpu.VMEM((SEQ_DEV, channels), jnp.bfloat16),
        in_specs=[NEAR] * 10,
        out_specs=NEAR,
        scratch_shapes=scratch(cells, channels, inner),
        cost_estimate=cost(cells, channels, inner),
        compiler_params=pltpu.CompilerParams(vmem_limit_bytes=24 << 20),
        name="encode_head",
    )(maps, *weights)


def pack_body(ahead, arrived, head, out, rows):
    half = head.shape[0]
    backlog = jnp.clip(jnp.sum(ahead[...]) // LANES, 0, half)
    for block in range(rows.shape[0]):
        lanes = slice(block * LANES, (block + 1) * LANES)
        rows[block, :half, :] = arrived[:, lanes].astype(jnp.float32)
        rows[block, half:, :] = head[:, lanes].astype(jnp.float32)
        out[:, lanes] = rows[block, pl.ds(half - backlog, half), :].astype(out.dtype)


def pack(ahead, arrived, head):
    return pl.pallas_call(
        pack_body,
        out_shape=jax.ShapeDtypeStruct(head.shape, head.dtype),
        in_specs=[NEAR] * 3,
        out_specs=NEAR,
        scratch_shapes=[pltpu.VMEM((head.shape[1] // LANES, 2 * head.shape[0], LANES), jnp.float32)],
        compiler_params=pltpu.CompilerParams(vmem_limit_bytes=4 << 20),
        name="pack",
    )(held(ahead), held(arrived), held(head))


def spread_body(where, count, out, again):
    again[...] = jnp.full(again.shape, count[0, 0])
    place = lax.broadcasted_iota(jnp.int32, out.shape, 0)
    out[...] = jnp.where(place > where[0, 0], count[0, 0] - SEQ_DEV, 0)


def spread(where, count, devices):
    return pl.pallas_call(
        spread_body,
        out_shape=[jax.ShapeDtypeStruct((devices, 1, LANES), jnp.int32), pltpu.VMEM((1, LANES), jnp.int32)],
        in_specs=[SCALAR] * 2,
        out_specs=[NEAR] * 2,
        cost_estimate=pl.CostEstimate(flops=10**11, bytes_accessed=10**8, transcendentals=0),
        compiler_params=pltpu.CompilerParams(vmem_limit_bytes=1 << 20),
        name="spread",
    )(where, count)


def on_device(tiles, tissue_index, tissue_count, w_reduce, s1, b1, w_spatial, s2, b2, w_expand, s3, b3):
    devices = lax.axis_size(AXES)
    rank = lax.axis_index(AXES).reshape(1, 1)
    count = tissue_count.reshape(1, 1)
    inner = w_reduce.shape[1]
    w_spatial = w_spatial.reshape(9 * inner, inner)
    w_reduce, s1, b1, s2, b2, s3, b3 = (
        held(v.reshape(-1, v.shape[-1])) for v in (w_reduce, s1, b1, s2, b2, s3, b3)
    )
    adds, count = spread(rank, count, devices)
    ahead = lax.all_to_all(adds, AXES, 0, 0, tiled=True)
    tail, maps, w_spatial, w_expand = encode_tail(
        tissue_index, count, tiles, w_reduce, s1, b1, w_spatial, s2, b2, w_expand, s3, b3
    )
    arrived = lax.ppermute(tail, AXES, [(i, i + 1) for i in range(devices - 1)])
    head = encode_head(maps, w_reduce, s1, b1, w_spatial, s2, b2, w_expand, s3, b3)
    return pack(ahead, arrived, head)


def solution(mesh):
    owned = P(AXES, None)
    return jax.shard_map(
        on_device,
        mesh=mesh,
        in_specs=(P(AXES, None, None), owned, P(AXES)) + (P(),) * 9,
        out_specs=owned,
        check_vma=False,
    )
```

```python
import jax
import jax.numpy as jnp
from jax import lax
from jax.experimental import pallas as pl
from jax.experimental.pallas import tpu as pltpu
from jax.sharding import PartitionSpec as P


SIDE = 7
SEQ_DEV = 8
LANES = 128
SUBLANES = 8
COLS = 256
AXES = ("grp", "ext")
SCALAR = pl.BlockSpec(memory_space=pltpu.SMEM)
NEAR = pl.BlockSpec(memory_space=pltpu.VMEM)
FAR = pl.BlockSpec(memory_space=pltpu.HBM)


def held(value):
    return pltpu.with_memory_space_constraint(value, pltpu.VMEM)


def encode(maps, weights, out, last_cell, by_cell, framed, spatial, partial, ready=lambda stage: None):
    w_reduce, scale_reduce, bias_reduce, w_spatial, scale_spatial, bias_spatial, w_expand, scale_expand, bias_expand = weights
    count, cells, channels = maps.shape
    inner = w_reduce.shape[1]
    even = cells - 1
    edge = jnp.zeros((SIDE, count, inner), framed.dtype)
    framed[:, :count, :] = edge
    framed[:, (SIDE + 1) * count :, :] = edge
    ready(0)
    for t in range(count):
        last_cell[t : t + 1, :] = maps[t, even:cells, :].astype(jnp.float32)
    x_last = last_cell[...].astype(jnp.bfloat16)
    rows = jnp.concatenate([maps[:, 0:even, :].reshape(count * even, channels), x_last], axis=0)
    for n in range(0, inner, COLS):
        cols = slice(n, n + COLS)
        grown = jnp.dot(rows, w_reduce[:, cols], preferred_element_type=jnp.float32)
        grown = jnp.maximum(grown * scale_reduce[:, cols] + bias_reduce[:, cols], 0.0)
        for q in range(COLS // LANES):
            block = n // LANES + q
            lanes = slice(q * LANES, (q + 1) * LANES)
            for t in range(count):
                by_cell[block, pl.ds(t, even, stride=count), :] = grown[t * even : (t + 1) * even, lanes]
            by_cell[block, even * count :, :] = grown[even * count :, lanes]
    for i in range(SIDE):
        for block in range(inner // LANES):
            framed[i, count : count + SIDE * count, block * LANES : (block + 1) * LANES] = by_cell[
                block, i * SIDE * count : (i + 1) * SIDE * count, :
            ].astype(jnp.bfloat16)
    ready(1)
    row_cells = SIDE * count
    for n in range(0, inner, COLS):
        cols = slice(n, n + COLS)
        parts = []
        for a in (1, 0, 2):
            first, final = max(0, a - 1), min(SIDE, SIDE + a - 1)
            windows = jnp.concatenate(
                [
                    framed[first:final, b * count : (b + SIDE) * count, :].reshape((final - first) * row_cells, inner)
                    for b in range(3)
                ],
                axis=1,
            )
            parts.append(
                jnp.dot(windows, w_spatial[a * 3 * inner : (a + 1) * 3 * inner, cols], preferred_element_type=jnp.float32)
            )
        middle, above, below = parts
        conv = jnp.concatenate(
            [
                middle[:row_cells] + below[:row_cells],
                middle[row_cells:-row_cells] + above[:-row_cells] + below[row_cells:],
                middle[-row_cells:] + above[-row_cells:],
            ],
            axis=0,
        )
        conv = jnp.maximum(conv * scale_spatial[:, cols] + bias_spatial[:, cols], 0.0)
        for q in range(COLS // LANES):
            by_cell[n // LANES + q, :, :] = conv[:, q * LANES : (q + 1) * LANES]
    for block in range(inner // LANES):
        lanes = slice(block * LANES, (block + 1) * LANES)
        for t in range(count):
            spatial[t * even : (t + 1) * even, lanes] = by_cell[block, pl.ds(t, even, stride=count), :].astype(
                jnp.bfloat16
            )
        spatial[even * count :, lanes] = by_cell[block, even * count :, :].astype(jnp.bfloat16)
    ready(2)
    for n in range(0, channels, COLS):
        cols = slice(n, n + COLS)
        grown = jnp.dot(spatial[...], w_expand[:, cols], preferred_element_type=jnp.float32)
        grown = grown * scale_expand[:, cols] + bias_expand[:, cols]
        most = grown[: even * count].reshape(count, even, COLS) + maps[:, 0:even, cols].astype(jnp.float32)
        last = grown[even * count :] + last_cell[:, cols]
        most = jnp.maximum(most, 0.0).reshape(count, even // SUBLANES, SUBLANES, COLS)
        part = jnp.sum(most, axis=1).reshape(count * SUBLANES, COLS)
        last = jnp.maximum(last, 0.0)
        for q in range(COLS // LANES):
            block = n // LANES + q
            lanes = slice(q * LANES, (q + 1) * LANES)
            partial[block, :, :] = part[:, lanes]
            total = last[:, lanes]
            for sub in range(SUBLANES):
                total = total + partial[block, pl.ds(sub, count, stride=SUBLANES), :]
            out[:, block * LANES : (block + 1) * LANES] = (total / cells).astype(out.dtype)


def scratch(cells, channels, inner):
    return [
        pltpu.VMEM((SEQ_DEV, channels), jnp.float32),
        pltpu.VMEM((inner // LANES, cells * SEQ_DEV, LANES), jnp.float32),
        pltpu.VMEM((SIDE, (SIDE + 2) * SEQ_DEV, inner), jnp.bfloat16),
        pltpu.VMEM((cells * SEQ_DEV, inner), jnp.bfloat16),
        pltpu.VMEM((channels // LANES, SEQ_DEV * SUBLANES, LANES), jnp.float32),
    ]


def cost(cells, channels, inner):
    return pl.CostEstimate(
        flops=2 * SEQ_DEV * cells * inner * (2 * channels + 9 * inner),
        bytes_accessed=2 * (SEQ_DEV * cells * channels + 2 * channels * inner + 9 * inner * inner),
        transcendentals=0,
    )


def tail_body(listing, count, tiles, w_spatial_far, w_expand_far, w_reduce, s1, b1, s2, b2, s3, b3, tail, head_maps, w_spatial, w_expand, maps, *rest):
    *work, sem = rest
    own = maps.shape[0]
    row = lax.broadcasted_iota(jnp.int32, (2 * own, listing.shape[1]), 0)
    lane = lax.broadcasted_iota(jnp.int32, (2 * own, listing.shape[1]), 1)
    amount = jnp.clip(count[:, : listing.shape[1]], 0, 2 * own)
    place = amount + own + row
    place = jnp.where(row < own, jnp.where(place >= 2 * own, place - 2 * own, place), row - own)
    place = jnp.where(place >= 2 * own, place - 2 * own, place)
    chosen = jnp.sum(jnp.where(lane == place, listing[...], 0), axis=1, keepdims=True)
    loads = []
    for t in range(own):
        loads.append(pltpu.make_async_copy(tiles.at[chosen[t, 0]], maps.at[t], sem.at[t]))
    later = [
        pltpu.make_async_copy(w_spatial_far, w_spatial, sem.at[own]),
        pltpu.make_async_copy(w_expand_far, w_expand, sem.at[own + 1]),
    ]
    later += [
        pltpu.make_async_copy(tiles.at[chosen[own + t, 0]], head_maps.at[t], sem.at[own + 2 + t]) for t in range(own)
    ]
    for copy in loads + later[:1]:
        copy.start()

    def ready(stage):
        if stage == 0:
            for copy in loads:
                copy.wait()
        else:
            later[stage - 1].wait()
        if stage == 1:
            for copy in later[1:]:
                copy.start()

    encode(maps, (w_reduce, s1, b1, w_spatial, s2, b2, w_expand, s3, b3), tail, *work, ready=ready)
    for copy in later[2:]:
        copy.wait()


def encode_tail(listing, count, tiles, w_reduce, s1, b1, w_spatial, s2, b2, w_expand, s3, b3):
    cells, channels = tiles.shape[1:]
    inner = w_reduce.shape[1]
    maps = (SEQ_DEV, cells, channels)
    return pl.pallas_call(
        tail_body,
        out_shape=[
            pltpu.VMEM((SEQ_DEV, channels), jnp.bfloat16),
            pltpu.VMEM(maps, tiles.dtype),
            pltpu.VMEM(w_spatial.shape, w_spatial.dtype),
            pltpu.VMEM(w_expand.shape, w_expand.dtype),
        ],
        in_specs=[NEAR] * 2 + [FAR] * 3 + [NEAR] * 7,
        out_specs=[NEAR] * 4,
        scratch_shapes=[pltpu.VMEM(maps, tiles.dtype)]
        + scratch(cells, channels, inner)
        + [pltpu.SemaphoreType.DMA((2 * SEQ_DEV + 2,))],
        cost_estimate=cost(cells, channels, inner),
        compiler_params=pltpu.CompilerParams(vmem_limit_bytes=40 << 20),
        name="encode_tail",
    )(held(listing), count, *(pltpu.with_memory_space_constraint(v, pltpu.HBM) for v in (tiles, w_spatial, w_expand)), w_reduce, s1, b1, s2, b2, s3, b3)


def head_body(maps, w_reduce, s1, b1, w_spatial, s2, b2, w_expand, s3, b3, head, *work):
    encode(maps, (w_reduce, s1, b1, w_spatial, s2, b2, w_expand, s3, b3), head, *work)


def encode_head(maps, *weights):
    cells, channels = maps.shape[1:]
    inner = weights[0].shape[1]
    return pl.pallas_call(
        head_body,
        out_shape=pltpu.VMEM((SEQ_DEV, channels), jnp.bfloat16),
        in_specs=[NEAR] * 10,
        out_specs=NEAR,
        scratch_shapes=scratch(cells, channels, inner),
        cost_estimate=cost(cells, channels, inner),
        compiler_params=pltpu.CompilerParams(vmem_limit_bytes=24 << 20),
        name="encode_head",
    )(maps, *weights)


def pack_body(ahead, arrived, head, out, rows):
    half = head.shape[0]
    backlog = jnp.clip(jnp.sum(ahead[...]) // LANES, 0, half)
    for block in range(rows.shape[0]):
        lanes = slice(block * LANES, (block + 1) * LANES)
        rows[block, :half, :] = arrived[:, lanes].astype(jnp.float32)
        rows[block, half:, :] = head[:, lanes].astype(jnp.float32)
        out[:, lanes] = rows[block, pl.ds(half - backlog, half), :].astype(out.dtype)


def pack(ahead, arrived, head):
    return pl.pallas_call(
        pack_body,
        out_shape=jax.ShapeDtypeStruct(head.shape, head.dtype),
        in_specs=[NEAR] * 3,
        out_specs=NEAR,
        scratch_shapes=[pltpu.VMEM((head.shape[1] // LANES, 2 * head.shape[0], LANES), jnp.float32)],
        compiler_params=pltpu.CompilerParams(vmem_limit_bytes=4 << 20),
        name="pack",
    )(held(ahead), held(arrived), held(head))


def spread_body(where, count, out, again):
    again[...] = jnp.full(again.shape, count[0, 0])
    place = lax.broadcasted_iota(jnp.int32, out.shape, 0)
    out[...] = jnp.where(place > where[0, 0], count[0, 0] - SEQ_DEV, 0)


def spread(where, count, devices):
    return pl.pallas_call(
        spread_body,
        out_shape=[jax.ShapeDtypeStruct((devices, 1, LANES), jnp.int32), pltpu.VMEM((1, LANES), jnp.int32)],
        in_specs=[SCALAR] * 2,
        out_specs=[NEAR] * 2,
        cost_estimate=pl.CostEstimate(flops=10**11, bytes_accessed=10**8, transcendentals=0),
        compiler_params=pltpu.CompilerParams(vmem_limit_bytes=1 << 20),
        name="spread",
    )(where, count)


def on_device(tiles, tissue_index, tissue_count, w_reduce, s1, b1, w_spatial, s2, b2, w_expand, s3, b3):
    devices = lax.axis_size(AXES)
    rank = lax.axis_index(AXES).reshape(1, 1)
    count = tissue_count.reshape(1, 1)
    inner = w_reduce.shape[1]
    w_spatial = w_spatial.reshape(9 * inner, inner)
    w_reduce, s1, b1, s2, b2, s3, b3 = (
        held(v.reshape(-1, v.shape[-1])) for v in (w_reduce, s1, b1, s2, b2, s3, b3)
    )
    adds, count = spread(rank, count, devices)
    ahead = lax.all_to_all(adds, AXES, 0, 0, tiled=True)
    tail, maps, w_spatial, w_expand = encode_tail(
        tissue_index, count, tiles, w_reduce, s1, b1, w_spatial, s2, b2, w_expand, s3, b3
    )
    arrived = lax.ppermute(tail, AXES, [(i, i + 1) for i in range(devices - 1)])
    head = encode_head(maps, w_reduce, s1, b1, w_spatial, s2, b2, w_expand, s3, b3)
    return pack(ahead, arrived, head)


def solution(mesh):
    owned = P(AXES, None)
    return jax.shard_map(
        on_device,
        mesh=mesh,
        in_specs=(P(AXES, None, None), owned, P(AXES)) + (P(),) * 9,
        out_specs=owned,
        check_vma=False,
    )
```
